32 devices in a mesh: groups: 2 (over y), seq: 4 (over z), head: 4 (over x, core).
Axes of the slice: x: 2, y: 2, z: 4, core: 2. Of those that a mesh axis runs over, the one named last changes fastest.
Arguments:
- hidden: bfloat16 [4096, 8192], P(('groups', 'seq')), parts along dimension 0, may hold values from -6 to 6
- w_in: bfloat16 [8192, 512], P('seq', 'head'), may hold values from -0.0625 to 0.0625
- decay_log: float32 [4096, 8], P(('groups', 'seq'), 'head'), parts along dimension 0, may hold values from -1 to 0
- b_proj: bfloat16 [4096, 4, 256], P(('groups', 'seq'), 'head'), parts along dimension 0, may hold values from -0.5 to 0.5
- c_proj: bfloat16 [4096, 4, 256], P(('groups', 'seq'), 'head'), parts along dimension 0, may hold values from -0.5 to 0.5
- grad_out: bfloat16 [4096, 512], P(('groups', 'seq'), 'head'), parts along dimension 0, may hold values from -0.079589844 to 0.079589844
Outputs:
- grad_w: float32 [16384, 512], P(('groups', 'seq'), 'head'), parts along dimension 0
- grad_decay: float32 [4096, 8], P(('groups', 'seq'), 'head'), parts along dimension 0
- grad_b: float32 [4096, 4, 256], P(('groups', 'seq'), 'head'), parts along dimension 0
- grad_c: float32 [4096, 4, 256], P(('groups', 'seq'), 'head'), parts along dimension 0
The draws below stay inside these ranges and needn't reach their ends.
There are 2 independent parts, one for each index of `groups`. The reference program is written for one: setup_inputs(seed, part) draws one part's arguments, and reference() takes and returns one part's arrays. A program takes and returns all parts, laid end to end along the dimension named above; an argument that names none is the same for every part. Nothing has to cross between parts.
All inputs are finite; a program needn't handle non-finite values.
Results may differ from the reference program's by a relative error of at most 0.0055.
Values may be sent and summed in bfloat16 or wider, within the bound.
No kernel may reach another device: no remote copies, remote signals or barrier semaphores. Data moves between devices by JAX's collectives and lax.ppermute only.
A program may use at most 128 MiB of HBM per device.

```python
import math
import jax
import jax.numpy as jnp
from jax import lax

D = 8192
HEAD_DIM = 64
STATE = 256
TOK_DEV = 512
HEADS = 8
GROUPS = 4
TOKENS = 2048


def draw_decay_log(key, part):
    keys = jax.random.split(jax.random.fold_in(key, 17), 7)
    slow_share = 0.5
    coins = jax.random.uniform(keys[0], (HEADS,))
    slow_rate = jnp.exp(jax.random.uniform(keys[1], (HEADS,), jnp.float32, math.log(0.1 / TOKENS), math.log(1.0 / TOKENS)))
    fast_rate = jnp.exp(jax.random.uniform(keys[2], (HEADS,), jnp.float32, math.log(1.0 / 50.0), math.log(1.0 / 20.0)))
    rate = jnp.where(coins < slow_share, slow_rate, fast_rate)
    jitter = jnp.exp(jax.random.uniform(keys[3], (TOKENS, HEADS), jnp.float32, math.log(0.5), math.log(2.0)))
    section_factor = jnp.exp(jax.random.uniform(keys[4], (TOKENS // TOK_DEV, 1, HEADS), jnp.float32, math.log(0.5), math.log(2.0)))
    section_factor = jnp.broadcast_to(section_factor, (TOKENS // TOK_DEV, TOK_DEV, HEADS)).reshape(TOKENS, HEADS)
    base = -(rate[None, :] * jitter * section_factor)
    places = jax.random.randint(keys[5], (3,), 0, TOKENS)
    struck = jnp.any(jnp.arange(TOKENS)[:, None] == places[None, :], axis=1)
    losses = jnp.log(jax.random.uniform(keys[6], (TOKENS, HEADS), jnp.float32, 0.55, 0.8))
    return (base + jnp.where(struck[:, None], losses, 0.0)).astype(jnp.float32)


def spiked(values, rng, source, target, parts, factor):
    owner, partner = [(jnp.arange(values.shape[dim]) // (values.shape[dim] // parts)).reshape([-1 if axis == dim else 1 for axis in range(values.ndim)]) for dim in (source, target)]
    chosen = jax.random.permutation(rng, parts)[partner]
    strong = (owner == chosen) | (owner == (partner + parts // 2) % parts)
    return jnp.where(strong, factor * values, values)


def level_of(rng, extent, cuts, low, top_value):
    loudness = 1.0
    for axis_at, shards_of in cuts:
        steps = jax.random.uniform(jax.random.fold_in(jax.random.fold_in(rng, 6), axis_at), (shards_of,), jnp.float32, low / len(cuts), top_value / len(cuts))
        loudness = loudness * jnp.repeat(jnp.exp(steps), extent[axis_at] // shards_of).reshape((-1,) + (1,) * (len(extent) - 1 - axis_at))
    return loudness


def noise(rng, extent, width, most, cuts=(), kind=jnp.bfloat16):
    gain = level_of(rng, extent, cuts, -0.22, 0.18) if cuts else 1.0
    values = jax.random.normal(rng, extent, jnp.float32) * width * gain
    return jnp.minimum(jnp.maximum(values, -most), most).astype(kind)


def bell_draw_with(key, dims, scale, reach, cuts, heavy, held_as=jnp.bfloat16):
    entries = scale * jax.random.normal(key, dims, jnp.float32)
    if cuts:
        entries = entries * level_of(key, dims, cuts, -0.22, 0.18)
    return jnp.clip(spiked(entries, jax.random.fold_in(key, 3), *heavy), -reach, reach).astype(held_as)


def setup_inputs(seed: int = 0, part: int = 0) -> dict:
    seeds = jax.random.split(jax.random.key(seed), 7)
    part_keys = jax.random.split(jax.random.fold_in(seeds[6], part), 7)
    return {
        "hidden": bell_draw_with(part_keys[0], (TOKENS, D), 1.0, 6.0, ((0, 4),), (0, 1, 4, 2.0)),
        "w_in": noise(seeds[1], (D, HEADS * HEAD_DIM), D ** -0.5, 0.0625, ((0, 4), (1, 4))),
        "decay_log": draw_decay_log(jax.random.fold_in(jax.random.fold_in(seeds[6], part), 71), part),
        "b_proj": noise(part_keys[3], (TOKENS, GROUPS, STATE), 0.0625, 0.5, ((0, 4), (1, 4))),
        "c_proj": noise(part_keys[4], (TOKENS, GROUPS, STATE), 0.0625, 0.5, ((0, 4), (1, 4))),
        "grad_out": noise(part_keys[5], (TOKENS, HEADS * HEAD_DIM), 0.01, 0.079589844, ((0, 4), (1, 4))),
    }


HIGHEST = lax.Precision.HIGHEST

def group_scores(c_rows, b_rows):
    return jnp.einsum('tgn,sgn->gts', c_rows.astype(jnp.bfloat16), b_rows.astype(jnp.bfloat16), preferred_element_type=jnp.float32)

def section_local(state_in, x_rows, log_decay, b_rows, c_rows, scores_group):
    length, head_count = log_decay.shape
    head_width = x_rows.shape[1] // head_count
    group_count = b_rows.shape[1]
    per_group = head_count // group_count
    running = jnp.cumsum(log_decay, axis=0)
    b_heads = jnp.repeat(b_rows, per_group, axis=1)
    c_heads = jnp.repeat(c_rows, per_group, axis=1)
    scores = jnp.repeat(scores_group, per_group, axis=0)
    spread = running.T[:, :, None] - running.T[:, None, :]
    causal = jnp.arange(length)[:, None] >= jnp.arange(length)[None, :]
    weights = jnp.exp(jnp.where(causal[None], spread, -jnp.inf))
    mixing = (scores * weights).astype(jnp.bfloat16)
    x_heads = x_rows.reshape(length, head_count, head_width)
    x_narrow = x_heads.astype(jnp.bfloat16)
    inner = jnp.einsum('hts,shp->thp', mixing, x_narrow, preferred_element_type=jnp.float32)
    state_heads = state_in.reshape(state_in.shape[0], head_count, head_width)
    carried = jnp.exp(running)[:, :, None] * jnp.einsum('thn,nhp->thp', c_heads, state_heads, precision=HIGHEST)
    output = (inner + carried).reshape(length, head_count * head_width)
    tail = jnp.exp(running[-1][None, :] - running)
    fresh = jnp.einsum('sh,shn,shp->nhp', tail, b_heads, x_heads, precision=HIGHEST)
    state_end = jnp.exp(running[-1])[None, :, None] * state_heads + fresh
    return (output, state_end.reshape(state_in.shape))

def section_grads(state_in, x_rows, log_decay, b_rows, c_rows, scores_group, upstream, grad_state):
    _, pullback = jax.vjp(section_local, state_in, x_rows, log_decay, b_rows, c_rows, scores_group)
    _, grad_proj, grad_log, grad_brow, grad_crow, grad_scores = pullback((upstream, grad_state))
    grad_crow = grad_crow + jnp.einsum('gts,sgn->tgn', grad_scores, b_rows, precision=HIGHEST)
    grad_brow = grad_brow + jnp.einsum('gts,tgn->sgn', grad_scores, c_rows, precision=HIGHEST)
    return (grad_proj, grad_log, grad_brow, grad_crow)

def section_decay(log_decay, head_width):
    running = jnp.cumsum(log_decay, axis=0)
    return jnp.repeat(jnp.exp(running[-1]), head_width)[None, :]

def section_start_grad(log_decay, c_rows, upstream):
    length, head_count = log_decay.shape
    head_width = upstream.shape[1] // head_count
    running = jnp.cumsum(log_decay, axis=0)
    c_heads = jnp.repeat(c_rows, head_count // c_rows.shape[1], axis=1)
    up_heads = upstream.reshape(length, head_count, head_width)
    start = jnp.einsum('thn,th,thp->nhp', c_heads, jnp.exp(running), up_heads, precision=HIGHEST)
    return start.reshape(c_rows.shape[2], head_count * head_width)

def reference(hidden, w_in, decay_log, b_proj, c_proj, grad_out):
    sections = TOKENS // TOK_DEV
    channels = HEADS * HEAD_DIM
    x_proj = jnp.dot(hidden, w_in, preferred_element_type=jnp.float32).astype(jnp.bfloat16)

    def split(array):
        return array.reshape((sections, TOK_DEV) + array.shape[1:])
    x_sec = split(x_proj).astype(jnp.float32)
    decay_sec = split(decay_log)
    b_sec = split(b_proj).astype(jnp.float32)
    c_sec = split(c_proj).astype(jnp.float32)
    up_sec = split(grad_out).astype(jnp.float32)
    zero_state = jnp.zeros((STATE, channels), jnp.float32)

    def elements(items):
        x_rows, log_decay, b_rows, c_rows, upstream = items
        scores_group = group_scores(c_rows, b_rows)
        fresh = section_local(zero_state, x_rows, log_decay, b_rows, c_rows, scores_group)[1]
        return (section_decay(log_decay, HEAD_DIM), fresh, section_start_grad(log_decay, c_rows, upstream))
    decays, fresh_all, start_all = lax.map(elements, (x_sec, decay_sec, b_sec, c_sec, up_sec))

    def forward_step(state, item):
        decay_now, fresh = item
        return (decay_now * state + fresh, state)
    _, state_start = lax.scan(forward_step, zero_state, (decays, fresh_all))

    def backward_step(grad_state, item):
        decay_now, start = item
        return (start + decay_now * grad_state, grad_state)
    _, grad_end = lax.scan(backward_step, zero_state, (decays, start_all), reverse=True)

    def gradients(items):
        state_in, grad_state, x_rows, log_decay, b_rows, c_rows, upstream = items
        scores_group = group_scores(c_rows, b_rows)
        return section_grads(state_in, x_rows, log_decay, b_rows, c_rows, scores_group, upstream, grad_state)
    grad_proj, grad_decay, grad_b, grad_c = lax.map(gradients, (state_start, grad_end, x_sec, decay_sec, b_sec, c_sec, up_sec))
    grad_x = grad_proj.reshape(TOKENS, channels).astype(jnp.bfloat16)
    grad_w = jnp.dot(hidden.T, grad_x, preferred_element_type=jnp.float32)
    return (grad_w, grad_decay.reshape(TOKENS, HEADS), grad_b.reshape(TOKENS, GROUPS, STATE), grad_c.reshape(TOKENS, GROUPS, STATE))
```

```python
import functools
import jax
import jax.numpy as jnp
from jax import lax
from jax.experimental import pallas as pl
from jax.experimental.pallas import tpu as pltpu
from jax.sharding import PartitionSpec as P

F32 = jnp.float32
BF16 = jnp.bfloat16
EXTRA = 16
BLOCK = 128


def params(limit=48):
    return pltpu.CompilerParams(vmem_limit_bytes=limit << 20)


def cost(flops, moved, exps=0):
    return pl.CostEstimate(flops=flops, bytes_accessed=moved, transcendentals=exps)


def dot(a, b, ca, cb):
    return lax.dot_general(a, b, (((ca,), (cb,)), ((), ())), preferred_element_type=F32)


def parts(x):
    high = x.astype(BF16)
    return high, (x - high.astype(F32)).astype(BF16)


def dot_left(x, b, ca, cb):
    high, low = parts(x)
    return dot(high, b, ca, cb) + dot(low, b, ca, cb)


def dot_right(a, x, ca, cb):
    high, low = parts(x)
    return dot(a, high, ca, cb) + dot(a, low, ca, cb)


def dot_full(x, y, ca, cb):
    xh, xl = parts(x)
    yh, yl = parts(y)
    return dot(xh, yh, ca, cb) + (dot(xh, yl, ca, cb) + dot(xl, yh, ca, cb))


def payload(state, last):
    high = last.astype(BF16).astype(F32)
    mid = (last - high).astype(BF16).astype(F32)
    low = last - high - mid
    row = lax.broadcasted_iota(jnp.int32, (EXTRA, last.shape[1]), 0)
    tail = jnp.where(row == 0, high, jnp.where(row == 1, mid, jnp.where(row == 2, low, 0.0)))
    return state.astype(BF16), tail.astype(BF16)


def combine(refs, rows):
    total = None
    for ref in reversed(refs):
        state = ref[0:rows, :].astype(F32)
        if total is not None:
            deep = ref[rows : rows + EXTRA, :].astype(F32)
            state = state + (deep[0:1] + deep[1:2] + deep[2:3]) * total
        total = state
    return total


def scan_lanes(x, reverse):
    length = x.shape[1]
    lane = lax.broadcasted_iota(jnp.int32, x.shape, 1)
    step = 1
    while step < length:
        if reverse:
            moved = jnp.where(lane < length - step, pltpu.roll(x, length - step, 1), 0.0)
        else:
            moved = jnp.where(lane >= step, pltpu.roll(x, step, 1), 0.0)
        x = x + moved
        step *= 2
    return x


def spread_rows(x, heads, rows):
    return jnp.concatenate(
        [jnp.broadcast_to(x[k : k + 1], (rows // heads, x.shape[1])) for k in range(heads)], axis=0
    )


def first_kernel(heads, decay_ref, c_ref, g_ref, pay_ref, run_ref, row_ref):
    channels = g_ref.shape[1]
    rows = scan_lanes(spread_rows(decay_ref[...], heads, 8), False)
    row_ref[...] = rows
    wide = jnp.concatenate(
        [jnp.broadcast_to(rows[k * 8 // heads : k * 8 // heads + 1], (channels // heads, rows.shape[1])) for k in range(heads)],
        axis=0,
    )
    run = wide.T
    run_ref[...] = run
    carried = jnp.exp(run) * g_ref[...].astype(F32)
    start = dot_right(c_ref[...], carried, 0, 0)
    state, tail = payload(start, jnp.exp(run[-1:, :]))
    n = state.shape[0]
    pay_ref[0:n, :] = state
    pay_ref[n : n + EXTRA, :] = tail


def weights(run, rows, k, heads, width, lo, hi, size):
    column = run[lo:hi, k * width : k * width + 1]
    line = rows[k * 8 // heads : k * 8 // heads + 1, lo:size]
    spread = line - column
    s = lax.broadcasted_iota(jnp.int32, spread.shape, 0)
    t = lax.broadcasted_iota(jnp.int32, spread.shape, 1)
    return jnp.exp(jnp.where(t >= s, spread, -jnp.inf))


def local_kernel(heads, b_ref, c_ref, g_ref, run_ref, row_ref, q_ref):
    size, channels = g_ref.shape
    width = channels // heads
    run, rows = run_ref[...], row_ref[...]
    for lo in range(0, size, BLOCK):
        hi = lo + BLOCK
        scores = dot(b_ref[lo:hi, :], c_ref[lo:size, :], 1, 1)
        out = []
        for k in range(heads):
            mixing = (scores * weights(run, rows, k, heads, width, lo, hi, size)).astype(BF16)
            out.append(dot(mixing, g_ref[lo:size, k * width : (k + 1) * width], 1, 0))
        q_ref[lo:hi, :] = jnp.concatenate(out, axis=1).astype(BF16)


def grad_x_kernel(count, *refs):
    pays, (b_ref, run_ref, q_ref), (ge_ref, bg_ref, gx_ref) = refs[:count], refs[count : count + 3], refs[count + 3 :]
    ge = combine(pays, ge_ref.shape[0])
    ge_ref[...] = ge
    bg = dot_right(b_ref[...], ge, 1, 0)
    bg_ref[...] = bg
    run = run_ref[...]
    tail = jnp.exp(run[-1:, :] - run)
    gx_ref[...] = (q_ref[...].astype(F32) + tail * bg).astype(BF16)


def chunk_kernel(adds, index_ref, hid_ref, gx_ref, *refs):
    total = dot(hid_ref[...], gx_ref[...], 0, 0)
    for ref in refs[:adds]:
        total = total + ref[...].astype(F32)
    refs[adds][...] = total.astype(refs[adds].dtype)


def fresh_payload(x, b, run, pay_ref):
    tail = jnp.exp(run[-1:, :] - run)
    fresh = dot_right(b, tail * x.astype(F32), 0, 0)
    state, extra = payload(fresh, jnp.exp(run[-1:, :]))
    n = state.shape[0]
    pay_ref[0:n, :] = state
    pay_ref[n : n + EXTRA, :] = extra


def proj_kernel(pieces, table_ref, hid_ref, b_ref, run_ref, *refs):
    w_refs, (x_ref, pay_ref, acc_ref) = refs[: len(pieces)], refs[len(pieces) :]
    step = pl.program_id(0)
    half = hid_ref.shape[1]
    at = 0
    for ref, count in zip(w_refs, pieces):
        for part in range(count):

            @pl.when(step == at)
            def _(ref=ref, part=part, at=at):
                product = dot(hid_ref[...], ref[part * half : (part + 1) * half, :], 1, 0)
                if at == 0:
                    acc_ref[...] = product
                else:
                    acc_ref[...] += product

            at += 1

    @pl.when(step == at - 1)
    def _():
        x = acc_ref[...].astype(BF16)
        x_ref[...] = x
        fresh_payload(x, b_ref[...], run_ref[...], pay_ref)


def fresh_kernel(x_ref, b_ref, run_ref, pay_ref):
    fresh_payload(x_ref[...], b_ref[...], run_ref[...], pay_ref)


def section_kernel(heads, b_ref, c_ref, g_ref, x_ref, run_ref, row_ref, ge_ref, bg_ref, gb_ref, gc_ref, gr_ref):
    size, channels = g_ref.shape
    width = channels // heads
    run, rows = run_ref[...], row_ref[...]
    x = x_ref[...].astype(F32)
    tail = jnp.exp(run[-1:, :] - run)
    moved = tail * x
    inner = moved * bg_ref[...]
    col = [[] for _ in range(heads)]
    line = [jnp.zeros((1, size), F32) for _ in range(heads)]
    gc_ref[...] = jnp.zeros_like(gc_ref)
    for lo in range(0, size, BLOCK):
        hi = lo + BLOCK
        scores = dot(b_ref[lo:hi, :], c_ref[lo:size, :], 1, 1)
        total = None
        for k in range(heads):
            ch = slice(k * width, (k + 1) * width)
            d_mix = dot(x_ref[lo:hi, ch], g_ref[lo:size, ch], 1, 1).astype(BF16).astype(F32)
            d_score = d_mix * weights(run, rows, k, heads, width, lo, hi, size)
            total = d_score if total is None else total + d_score
            z = d_score * scores
            col[k].append(jnp.sum(z, axis=1, keepdims=True))
            above = jnp.sum(z, axis=0, keepdims=True)
            if lo:
                above = jnp.concatenate([jnp.zeros((1, lo), F32), above], axis=1)
            line[k] = line[k] + above
        high, low = parts(total)
        gb_ref[lo:hi, :] = dot(high, c_ref[lo:size, :], 1, 0) + dot(low, c_ref[lo:size, :], 1, 0)
        gc_ref[lo:size, :] += dot(high, b_ref[lo:hi, :], 0, 0) + dot(low, b_ref[lo:hi, :], 0, 0)
    gb_ref[...] += dot_full(moved, ge_ref[...], 1, 1)
    taken, ends = [], []
    for k in range(heads):
        fade = jnp.sum(inner[:, k * width : (k + 1) * width], axis=1, keepdims=True)
        ends.append(jnp.sum(fade, axis=0, keepdims=True))
        taken.append(jnp.broadcast_to(jnp.concatenate(col[k], axis=0) + fade, (size, width)))
    flipped = jnp.concatenate(taken, axis=1).T
    lane = lax.broadcasted_iota(jnp.int32, (1, size), 1)
    for k in range(heads):
        value = line[k] - flipped[k * width : k * width + 1, :]
        value = value + jnp.where(lane == size - 1, ends[k], 0.0)
        gr_ref[k * 8 // heads : (k + 1) * 8 // heads, :] = jnp.broadcast_to(value, (8 // heads, size))


def last_kernel(heads, count, *refs):
    pays = refs[:count]
    c_ref, g_ref, run_ref, ge_ref, gc_ref, gr_ref, out_ref, gd_ref = refs[count:]
    size, channels = g_ref.shape
    width = channels // heads
    state = combine(pays, ge_ref.shape[0])
    run = run_ref[...]
    carried = jnp.exp(run) * g_ref[...].astype(F32)
    out_ref[...] = gc_ref[...] + dot_full(carried, state, 1, 1)
    inner = carried * dot_right(c_ref[...], state, 1, 0)
    ends = jnp.exp(run[-1:, :]) * jnp.sum(ge_ref[...] * state, axis=0, keepdims=True)
    taken, last = [], []
    for k in range(heads):
        ch = slice(k * width, (k + 1) * width)
        taken.append(jnp.broadcast_to(jnp.sum(inner[:, ch], axis=1, keepdims=True), (size, width)))
        last.append(jnp.broadcast_to(jnp.sum(ends[:, ch], axis=1, keepdims=True), (8 // heads, 1)))
    flipped = jnp.concatenate(taken, axis=1).T
    lines = jnp.concatenate(
        [jnp.broadcast_to(flipped[k * width : k * width + 1, :], (8 // heads, size)) for k in range(heads)], axis=0
    )
    lane = lax.broadcasted_iota(jnp.int32, (8, size), 1)
    lines = lines + gr_ref[...] + jnp.where(lane == size - 1, jnp.concatenate(last, axis=0), 0.0)
    total = scan_lanes(lines, True)
    for k in range(heads):
        gd_ref[k : k + 1, :] = total[k * 8 // heads : k * 8 // heads + 1, :]


def shift(x, count, k):
    return lax.ppermute(x, "seq", [(i, i + k) for i in range(count) if 0 <= i + k < count])


def chunk(hidden, gx, index, rows, dtype, adds=(), step=512):
    size, channels = gx.shape
    step = min(step, rows)
    blocks = rows // step
    return pl.pallas_call(
        functools.partial(chunk_kernel, len(adds)),
        grid_spec=pltpu.PrefetchScalarGridSpec(
            num_scalar_prefetch=1,
            grid=(blocks,),
            in_specs=[
                pl.BlockSpec((size, step), lambda i, s: (0, s[0] * blocks + i)),
                pl.BlockSpec((size, channels), lambda i, s: (0, 0)),
            ]
            + [pl.BlockSpec((step, channels), lambda i, s: (i, 0)) for _ in adds],
            out_specs=pl.BlockSpec((step, channels), lambda i, s: (i, 0)),
        ),
        out_shape=jax.ShapeDtypeStruct((rows, channels), dtype),
        compiler_params=params(),
        cost_estimate=cost(2 * size * rows * channels, size * rows * 2 + rows * channels * 4),
    )(index, hidden, gx, *adds)


def body(hidden, w_in, decay_log, b_proj, c_proj, grad_out):
    count = lax.axis_size("seq")
    place = lax.axis_index("seq")
    side = lax.axis_index("groups")
    size, heads = decay_log.shape
    channels = w_in.shape[1]
    states = b_proj.shape[2]
    share = w_in.shape[0]
    b = b_proj.reshape(size, states)
    c = c_proj.reshape(size, states)
    f32 = lambda *s: jax.ShapeDtypeStruct(s, F32)
    b16 = lambda *s: jax.ShapeDtypeStruct(s, BF16)

    pay, run, rows = pl.pallas_call(
        functools.partial(first_kernel, heads),
        out_shape=(b16(states + EXTRA, channels), f32(size, channels), f32(8, size)),
        compiler_params=params(),
        cost_estimate=cost(4 * size * states * channels, 1 << 20),
    )(decay_log.T, c, grad_out)
    later = [shift(pay, count, -k) for k in range(1, count)]

    direct = count == 4 and lax.axis_size("groups") == 2
    if direct:
        half = share // 2
        mine = lax.dynamic_slice_in_dim(w_in, side * half, half, 0)
        moved = [
            lax.ppermute(mine, "seq", [(i, (i + k) % count) for i in range(count)]) for k in (2, 1, 3)
        ]
        other = [lax.ppermute(m, "groups", [(0, 1), (1, 0)]) for m in moved]

    q = pl.pallas_call(
        functools.partial(local_kernel, heads),
        out_shape=b16(size, channels),
        compiler_params=params(),
        cost_estimate=cost(2 * size * size * (states + channels), 1 << 20, size * size * heads),
    )(b, c, grad_out, run, rows)
    ge, bg, gx = pl.pallas_call(
        functools.partial(grad_x_kernel, count - 1),
        out_shape=(f32(states, channels), f32(size, channels), b16(size, channels)),
        compiler_params=params(),
        cost_estimate=cost(4 * size * states * channels, 1 << 20),
    )(*later, b, run, q)

    if direct:
        pick = lambda t: jnp.reshape(t, (1,)).astype(jnp.int32)
        near = [(i, i ^ 1) for i in range(count)]
        far = [(i, i ^ 2) for i in range(count)]
        send_a = chunk(hidden, gx, pick(place ^ 3), share, BF16)
        got_a = lax.ppermute(send_a, "seq", near)
        send_b = chunk(hidden, gx, pick(place ^ 1), share, BF16)
        got_b = lax.ppermute(send_b, "seq", near)
        send_c = chunk(hidden, gx, pick(place ^ 2), share, BF16, (got_a,))
        got_c = lax.ppermute(send_c, "seq", far)
        own = chunk(hidden, gx, pick(place), share, F32)
        grad_w = own + got_b.astype(F32) + got_c.astype(F32)

        sources = [place] + [(place - k) % count for k in (2, 1, 3)]
        table = [2 * place, 2 * place + 1]
        table += [2 * s + side for s in sources[1:]] + [2 * s + 1 - side for s in sources[1:]]
        table = jnp.stack(table).astype(jnp.int32)
        pieces = (2, 1, 1, 1, 1, 1, 1)
        whole = lambda i, s: (0, 0)
        x, pay_x = pl.pallas_call(
            functools.partial(proj_kernel, pieces),
            grid_spec=pltpu.PrefetchScalarGridSpec(
                num_scalar_prefetch=1,
                grid=(sum(pieces),),
                in_specs=[
                    pl.BlockSpec((size, half), lambda i, s: (0, s[i])),
                    pl.BlockSpec((size, states), whole),
                    pl.BlockSpec((size, channels), whole),
                    pl.BlockSpec((share, channels), whole),
                ]
                + [pl.BlockSpec((half, channels), whole)] * 6,
                out_specs=[
                    pl.BlockSpec((size, channels), whole),
                    pl.BlockSpec((states + EXTRA, channels), whole),
                ],
                scratch_shapes=[pltpu.VMEM((size, channels), F32)],
            ),
            out_shape=(b16(size, channels), b16(states + EXTRA, channels)),
            compiler_params=params(),
            cost_estimate=cost(2 * size * hidden.shape[1] * channels, 10 << 20),
        )(table, hidden, b, run, w_in, *moved, *other)
    else:
        grad_w = lax.psum_scatter(
            lax.dot_general(hidden, gx, (((0,), (0,)), ((), ())), preferred_element_type=F32),
            "seq",
            scatter_dimension=0,
            tiled=True,
        )
        w_all = lax.all_gather(w_in, "seq", axis=0, tiled=True)
        x = jnp.dot(hidden, w_all, preferred_element_type=F32).astype(BF16)
        pay_x = pl.pallas_call(
            fresh_kernel, out_shape=b16(states + EXTRA, channels), compiler_params=params()
        )(x, b, run)

    earlier = [shift(pay_x, count, k) for k in range(1, count)]
    grad_b, gc_part, gr_part = pl.pallas_call(
        functools.partial(section_kernel, heads),
        out_shape=(f32(size, states), f32(size, states), f32(8, size)),
        compiler_params=params(),
        cost_estimate=cost(6 * size * size * (states + channels), 3 << 20, size * size * heads),
    )(b, c, grad_out, x, run, rows, ge, bg)
    grad_c, grad_decay = pl.pallas_call(
        functools.partial(last_kernel, heads, count - 1),
        out_shape=(f32(size, states), f32(heads, size)),
        compiler_params=params(),
        cost_estimate=cost(10 * size * states * channels, 2 << 20),
    )(*earlier, c, grad_out, run, ge, gc_part, gr_part)
    return (
        grad_w,
        grad_decay.T,
        grad_b.reshape(size, 1, states),
        grad_c.reshape(size, 1, states),
    )


def solution(mesh):
    return jax.shard_map(
        body,
        mesh=mesh,
        in_specs=(
            P(("groups", "seq"), None),
            P("seq", "head"),
            P(("groups", "seq"), "head"),
            P(("groups", "seq"), "head", None),
            P(("groups", "seq"), "head", None),
            P(("groups", "seq"), "head"),
        ),
        out_specs=(
            P(("groups", "seq"), "head"),
            P(("groups", "seq"), "head"),
            P(("groups", "seq"), "head", None),
            P(("groups", "seq"), "head", None),
        ),
        check_vma=False,
    )
```

```python
import functools
import jax
import jax.numpy as jnp
from jax import lax
from jax.experimental import pallas as pl
from jax.experimental.pallas import tpu as pltpu
from jax.sharding import PartitionSpec as P

F32 = jnp.float32
BF16 = jnp.bfloat16
EXTRA = 16
BLOCK = 128


def params(limit=12):
    return pltpu.CompilerParams(vmem_limit_bytes=limit << 20)


def cost(flops, moved, exps=0):
    return pl.CostEstimate(flops=flops, bytes_accessed=moved, transcendentals=exps)


def dot(a, b, ca, cb):
    return lax.dot_general(a, b, (((ca,), (cb,)), ((), ())), preferred_element_type=F32)


def parts(x):
    high = x.astype(BF16)
    return high, (x - high.astype(F32)).astype(BF16)


def dot_left(x, b, ca, cb):
    high, low = parts(x)
    return dot(high, b, ca, cb) + dot(low, b, ca, cb)


def dot_right(a, x, ca, cb):
    high, low = parts(x)
    return dot(a, high, ca, cb) + dot(a, low, ca, cb)


def dot_full(x, y, ca, cb):
    xh, xl = parts(x)
    yh, yl = parts(y)
    return dot(xh, yh, ca, cb) + (dot(xh, yl, ca, cb) + dot(xl, yh, ca, cb))


def payload(state, last):
    high = last.astype(BF16).astype(F32)
    mid = (last - high).astype(BF16).astype(F32)
    low = last - high - mid
    row = lax.broadcasted_iota(jnp.int32, (EXTRA, last.shape[1]), 0)
    tail = jnp.where(row == 0, high, jnp.where(row == 1, mid, jnp.where(row == 2, low, 0.0)))
    return state.astype(BF16), tail.astype(BF16)


def combine(refs, rows):
    total = None
    for ref in reversed(refs):
        state = ref[0:rows, :].astype(F32)
        if total is not None:
            deep = ref[rows : rows + EXTRA, :].astype(F32)
            state = state + (deep[0:1] + deep[1:2] + deep[2:3]) * total
        total = state
    return total


def scan_lanes(x, reverse):
    length = x.shape[1]
    lane = lax.broadcasted_iota(jnp.int32, x.shape, 1)
    step = 1
    while step < length:
        if reverse:
            moved = jnp.where(lane < length - step, pltpu.roll(x, length - step, 1), 0.0)
        else:
            moved = jnp.where(lane >= step, pltpu.roll(x, step, 1), 0.0)
        x = x + moved
        step *= 2
    return x


def spread_rows(x, heads, rows):
    return jnp.concatenate(
        [jnp.broadcast_to(x[k : k + 1], (rows // heads, x.shape[1])) for k in range(heads)], axis=0
    )


def first_kernel(heads, decay_ref, c_hbm, g_hbm, w_hbm, pay_ref, run_ref, row_ref, c_ref, g_ref, w_ref, sems):
    half = w_ref.shape[0]
    side = lax.axis_index("groups") if half < w_hbm.shape[0] else 0
    copies = [
        pltpu.make_async_copy(w_hbm.at[pl.ds(pl.multiple_of(side * half, half), half), :], w_ref, sems.at[2]),
        pltpu.make_async_copy(c_hbm, c_ref, sems.at[0]),
        pltpu.make_async_copy(g_hbm, g_ref, sems.at[1]),
    ]
    for copy in copies:
        copy.start()
    channels = g_ref.shape[1]
    rows = scan_lanes(spread_rows(decay_ref[...], heads, 8), False)
    row_ref[...] = rows
    wide = jnp.concatenate(
        [jnp.broadcast_to(rows[k * 8 // heads : k * 8 // heads + 1], (channels // heads, rows.shape[1])) for k in range(heads)],
        axis=0,
    )
    run = wide.T
    run_ref[...] = run
    for copy in copies:
        copy.wait()
    carried = jnp.exp(run) * g_ref[...].astype(F32)
    start = dot_right(c_ref[...], carried, 0, 0)
    state, tail = payload(start, jnp.exp(run[-1:, :]))
    n = state.shape[0]
    pay_ref[0:n, :] = state
    pay_ref[n : n + EXTRA, :] = tail


def weights(run, rows, k, heads, width, lo, hi, size):
    column = run[lo:hi, k * width : k * width + 1]
    line = rows[k * 8 // heads : k * 8 // heads + 1, lo:size]
    spread = line - column
    s = lax.broadcasted_iota(jnp.int32, spread.shape, 0)
    t = lax.broadcasted_iota(jnp.int32, spread.shape, 1)
    return jnp.exp(jnp.where(t >= s, spread, -jnp.inf))


def local_kernel(heads, b_ref, c_ref, g_ref, run_ref, row_ref, q_ref):
    size, channels = g_ref.shape
    width = channels // heads
    run, rows = run_ref[...], row_ref[...]
    for lo in range(0, size, BLOCK):
        hi = lo + BLOCK
        scores = dot(b_ref[lo:hi, :], c_ref[lo:size, :], 1, 1)
        out = []
        for k in range(heads):
            mixing = (scores * weights(run, rows, k, heads, width, lo, hi, size)).astype(BF16)
            out.append(dot(mixing, g_ref[lo:size, k * width : (k + 1) * width], 1, 0))
        q_ref[lo:hi, :] = jnp.concatenate(out, axis=1).astype(BF16)


def product(hid_ref, gx, index, rows):
    block = hid_ref[:, pl.ds(pl.multiple_of(index * rows, rows), rows)]
    return dot(gx, block, 0, 0).T


def grad_x_kernel(count, flip, hid_ref, *refs):
    pays, (b_ref, run_ref, q_ref), (ge_ref, bg_ref, gx_ref, out_ref) = (
        refs[:count],
        refs[count : count + 3],
        refs[count + 3 :],
    )
    ge = combine(pays, ge_ref.shape[0])
    ge_ref[...] = ge
    bg = dot_right(b_ref[...], ge, 1, 0)
    bg_ref[...] = bg
    run = run_ref[...]
    tail = jnp.exp(run[-1:, :] - run)
    gx = (q_ref[...].astype(F32) + tail * bg).astype(BF16)
    gx_ref[...] = gx
    out_ref[...] = product(hid_ref, gx, lax.axis_index("seq") ^ flip, out_ref.shape[0]).astype(out_ref.dtype)


def chunk_kernel(adds, flip, hid_ref, gx_ref, *refs):
    total = product(hid_ref, gx_ref[...], lax.axis_index("seq") ^ flip, refs[adds].shape[0])
    for ref in refs[:adds]:
        total = total + ref[...].astype(F32)
    refs[adds][...] = total.astype(refs[adds].dtype)


def fresh_payload(x, b, run, pay_ref):
    tail = jnp.exp(run[-1:, :] - run)
    fresh = dot_right(b, tail * x.astype(F32), 0, 0)
    state, extra = payload(fresh, jnp.exp(run[-1:, :]))
    n = state.shape[0]
    pay_ref[0:n, :] = state
    pay_ref[n : n + EXTRA, :] = extra


def proj_kernel(hops, swapped, last, hid_ref, *refs):
    count = len(hops)
    place, side, sections = lax.axis_index("seq"), lax.axis_index("groups"), lax.axis_size("seq")
    w_refs, rest = refs[:count], refs[count:]
    total = None if not last else rest[0][...]
    for ref, hop in zip(w_refs, hops):
        width = ref.shape[0]
        if hop == 0:
            at = place
        else:
            at = 2 * lax.rem(place - hop + sections, sections) + (1 - side if swapped else side)
        block = hid_ref[:, pl.ds(pl.multiple_of(at * width, width), width)]
        term = dot(block, ref[...], 1, 0)
        total = term if total is None else total + term
    if not last:
        rest[0][...] = total
    else:
        b_ref, run_ref, x_ref, pay_ref = rest[1:]
        x = total.astype(BF16)
        x_ref[...] = x
        fresh_payload(x, b_ref[...], run_ref[...], pay_ref)


def fresh_kernel(x_ref, b_ref, run_ref, pay_ref):
    fresh_payload(x_ref[...], b_ref[...], run_ref[...], pay_ref)


def section_kernel(heads, b_ref, c_ref, g_ref, x_ref, run_ref, row_ref, ge_ref, bg_ref, gb_ref, gc_ref, gr_ref):
    size, channels = g_ref.shape
    width = channels // heads
    run, rows = run_ref[...], row_ref[...]
    x = x_ref[...].astype(F32)
    tail = jnp.exp(run[-1:, :] - run)
    moved = tail * x
    inner = moved * bg_ref[...]
    col = [[] for _ in range(heads)]
    line = [jnp.zeros((1, size), F32) for _ in range(heads)]
    gc_ref[...] = jnp.zeros_like(gc_ref)
    for lo in range(0, size, BLOCK):
        hi = lo + BLOCK
        scores = dot(b_ref[lo:hi, :], c_ref[lo:size, :], 1, 1)
        total = None
        for k in range(heads):
            ch = slice(k * width, (k + 1) * width)
            d_mix = dot(x_ref[lo:hi, ch], g_ref[lo:size, ch], 1, 1).astype(BF16).astype(F32)
            d_score = d_mix * weights(run, rows, k, heads, width, lo, hi, size)
            total = d_score if total is None else total + d_score
            z = d_score * scores
            col[k].append(jnp.sum(z, axis=1, keepdims=True))
            above = jnp.sum(z, axis=0, keepdims=True)
            if lo:
                above = jnp.concatenate([jnp.zeros((1, lo), F32), above], axis=1)
            line[k] = line[k] + above
        high, low = parts(total)
        gb_ref[lo:hi, :] = dot(high, c_ref[lo:size, :], 1, 0) + dot(low, c_ref[lo:size, :], 1, 0)
        gc_ref[lo:size, :] += dot(high, b_ref[lo:hi, :], 0, 0) + dot(low, b_ref[lo:hi, :], 0, 0)
    gb_ref[...] += dot_full(moved, ge_ref[...], 1, 1)
    taken, ends = [], []
    for k in range(heads):
        fade = jnp.sum(inner[:, k * width : (k + 1) * width], axis=1, keepdims=True)
        ends.append(jnp.sum(fade, axis=0, keepdims=True))
        taken.append(jnp.broadcast_to(jnp.concatenate(col[k], axis=0) + fade, (size, width)))
    flipped = jnp.concatenate(taken, axis=1).T
    lane = lax.broadcasted_iota(jnp.int32, (1, size), 1)
    for k in range(heads):
        value = line[k] - flipped[k * width : k * width + 1, :]
        value = value + jnp.where(lane == size - 1, ends[k], 0.0)
        gr_ref[k * 8 // heads : (k + 1) * 8 // heads, :] = jnp.broadcast_to(value, (8 // heads, size))


def last_kernel(heads, count, *refs):
    pays = refs[:count]
    c_ref, g_ref, run_ref, ge_ref, gc_ref, gr_ref, out_ref, gd_ref = refs[count:]
    size, channels = g_ref.shape
    width = channels // heads
    state = combine(pays, ge_ref.shape[0])
    run = run_ref[...]
    carried = jnp.exp(run) * g_ref[...].astype(F32)
    out_ref[...] = gc_ref[...] + dot_full(carried, state, 1, 1)
    inner = carried * dot_right(c_ref[...], state, 1, 0)
    ends = jnp.exp(run[-1:, :]) * jnp.sum(ge_ref[...] * state, axis=0, keepdims=True)
    taken, last = [], []
    for k in range(heads):
        ch = slice(k * width, (k + 1) * width)
        taken.append(jnp.broadcast_to(jnp.sum(inner[:, ch], axis=1, keepdims=True), (size, width)))
        last.append(jnp.broadcast_to(jnp.sum(ends[:, ch], axis=1, keepdims=True), (8 // heads, 1)))
    flipped = jnp.concatenate(taken, axis=1).T
    lines = jnp.concatenate(
        [jnp.broadcast_to(flipped[k * width : k * width + 1, :], (8 // heads, size)) for k in range(heads)], axis=0
    )
    lane = lax.broadcasted_iota(jnp.int32, (8, size), 1)
    lines = lines + gr_ref[...] + jnp.where(lane == size - 1, jnp.concatenate(last, axis=0), 0.0)
    total = scan_lanes(lines, True)
    for k in range(heads):
        gd_ref[k : k + 1, :] = total[k * 8 // heads : k * 8 // heads + 1, :]


def shift(x, count, k):
    return lax.ppermute(x, "seq", [(i, i + k) for i in range(count) if 0 <= i + k < count])


def on_chip(kernel, shapes, flops, *args, far=(), copies=0):
    spaces = [pl.ANY if i in far else pltpu.VMEM for i in range(len(args))]
    many = isinstance(shapes, (list, tuple))
    vmem = pl.BlockSpec(memory_space=pltpu.VMEM)
    return pl.pallas_call(
        kernel,
        in_specs=[pl.BlockSpec(memory_space=m) for m in spaces],
        out_specs=[vmem] * len(shapes) if many else vmem,
        out_shape=list(shapes) if many else shapes,
        scratch_shapes=[pltpu.SemaphoreType.DMA((copies,))] if copies else [],
        compiler_params=params(),
        cost_estimate=cost(int(flops * 1.1e9), 1 << 10),
    )(*args)


def body(hidden, w_in, decay_log, b_proj, c_proj, grad_out):
    count = lax.axis_size("seq")
    size, heads = decay_log.shape
    channels = w_in.shape[1]
    states = b_proj.shape[2]
    share = w_in.shape[0]
    b = b_proj.reshape(size, states)
    c = c_proj.reshape(size, states)
    f32 = lambda *s: jax.ShapeDtypeStruct(s, F32)
    b16 = lambda *s: jax.ShapeDtypeStruct(s, BF16)

    direct = count == 4 and lax.axis_size("groups") == 2
    half = share // 2 if direct else share
    pay, run, rows, c, g, mine = on_chip(
        functools.partial(first_kernel, heads),
        (
            b16(states + EXTRA, channels),
            f32(size, channels),
            f32(8, size),
            b16(size, states),
            b16(size, channels),
            b16(half, channels),
        ),
        1.2, decay_log.T, c, grad_out, w_in, far=(1, 2, 3), copies=3,
    )
    later = [shift(pay, count, -k) for k in range(1, count)]

    if direct:
        hops = (2, 1, 3)
        moved = [lax.ppermute(mine, "seq", [(i, (i + k) % count) for i in range(count)]) for k in hops]
        other = [lax.ppermute(m, "groups", [(0, 1), (1, 0)]) for m in moved]

    q = on_chip(functools.partial(local_kernel, heads), b16(size, channels), 1.1, b, c, g, run, rows)
    ge, bg, gx, send_a = on_chip(
        functools.partial(grad_x_kernel, count - 1, 3 if direct else 0),
        (f32(states, channels), f32(size, channels), b16(size, channels), b16(share, channels)),
        8.0, hidden, *later, b, run, q,
    )

    if direct:
        near = [(i, i ^ 1) for i in range(count)]
        far = [(i, i ^ 2) for i in range(count)]
        chunk = lambda flip, dtype, price, *adds: on_chip(
            functools.partial(chunk_kernel, len(adds), flip),
            jax.ShapeDtypeStruct((share, channels), dtype),
            price, hidden, gx, *adds,
        )
        got_a = lax.ppermute(send_a, "seq", near)
        send_b = chunk(1, BF16, 6.0)
        got_b = lax.ppermute(send_b, "seq", near)
        send_c = chunk(2, BF16, 6.0, got_a)
        got_c = lax.ppermute(send_c, "seq", far)
        own = chunk(0, F32, 0.55, got_b)
        grad_w = own + got_c.astype(F32)

        acc = on_chip(
            functools.partial(proj_kernel, (0,) + hops, False, False),
            f32(size, channels),
            1.5, hidden, w_in, *moved,
        )
        x, pay_x = on_chip(
            functools.partial(proj_kernel, hops, True, True),
            (b16(size, channels), b16(states + EXTRA, channels)),
            1.5, hidden, *other, acc, b, run,
        )
    else:
        grad_w = lax.psum_scatter(
            lax.dot_general(hidden, gx, (((0,), (0,)), ((), ())), preferred_element_type=F32),
            "seq",
            scatter_dimension=0,
            tiled=True,
        )
        w_all = lax.all_gather(w_in, "seq", axis=0, tiled=True)
        x = jnp.dot(hidden, w_all, preferred_element_type=F32).astype(BF16)
        pay_x = on_chip(fresh_kernel, b16(states + EXTRA, channels), 1.0, x, b, run)

    earlier = [shift(pay_x, count, k) for k in range(1, count)]
    grad_b, gc_part, gr_part = on_chip(
        functools.partial(section_kernel, heads),
        (f32(size, states), f32(size, states), f32(8, size)),
        1.8, b, c, g, x, run, rows, ge, bg,
    )
    grad_c, grad_decay = on_chip(
        functools.partial(last_kernel, heads, count - 1),
        (f32(size, states), f32(heads, size)),
        2.6, *earlier, c, g, run, ge, gc_part, gr_part,
    )
    return (
        grad_w,
        grad_decay.T,
        grad_b.reshape(size, 1, states),
        grad_c.reshape(size, 1, states),
    )


def solution(mesh):
    return jax.shard_map(
        body,
        mesh=mesh,
        in_specs=(
            P(("groups", "seq"), None),
            P("seq", "head"),
            P(("groups", "seq"), "head"),
            P(("groups", "seq"), "head", None),
            P(("groups", "seq"), "head", None),
            P(("groups", "seq"), "head"),
        ),
        out_specs=(
            P(("groups", "seq"), "head"),
            P(("groups", "seq"), "head"),
            P(("groups", "seq"), "head", None),
            P(("groups", "seq"), "head", None),
        ),
        check_vma=False,
    )
```

```python
import functools
import jax
import jax.numpy as jnp
from jax import lax
from jax.experimental import pallas as pl
from jax.experimental.pallas import tpu as pltpu
from jax.sharding import PartitionSpec as P

F32 = jnp.float32
BF16 = jnp.bfloat16
EXTRA = 16
BLOCK = 128


def params(limit=12):
    return pltpu.CompilerParams(vmem_limit_bytes=limit << 20)


def cost(flops, moved, exps=0):
    return pl.CostEstimate(flops=flops, bytes_accessed=moved, transcendentals=exps)


def dot(a, b, ca, cb):
    return lax.dot_general(a, b, (((ca,), (cb,)), ((), ())), preferred_element_type=F32)


def parts(x):
    high = x.astype(BF16)
    return high, (x - high.astype(F32)).astype(BF16)


def dot_left(x, b, ca, cb):
    high, low = parts(x)
    return dot(high, b, ca, cb) + dot(low, b, ca, cb)


def dot_right(a, x, ca, cb):
    high, low = parts(x)
    return dot(a, high, ca, cb) + dot(a, low, ca, cb)


def dot_full(x, y, ca, cb):
    xh, xl = parts(x)
    yh, yl = parts(y)
    return dot(xh, yh, ca, cb) + (dot(xh, yl, ca, cb) + dot(xl, yh, ca, cb))


def payload(state, last):
    high = last.astype(BF16).astype(F32)
    mid = (last - high).astype(BF16).astype(F32)
    low = last - high - mid
    row = lax.broadcasted_iota(jnp.int32, (EXTRA, last.shape[1]), 0)
    tail = jnp.where(row == 0, high, jnp.where(row == 1, mid, jnp.where(row == 2, low, 0.0)))
    return state.astype(BF16), tail.astype(BF16)


def combine(refs, rows):
    total = None
    for ref in reversed(refs):
        state = ref[0:rows, :].astype(F32)
        if total is not None:
            deep = ref[rows : rows + EXTRA, :].astype(F32)
            state = state + (deep[0:1] + deep[1:2] + deep[2:3]) * total
        total = state
    return total


def scan_lanes(x, reverse):
    row = lax.broadcasted_iota(jnp.int32, (BLOCK, BLOCK), 0)
    lane = lax.broadcasted_iota(jnp.int32, (BLOCK, BLOCK), 1)
    ones = jnp.where(row >= lane if reverse else row <= lane, 1.0, 0.0).astype(BF16)
    high, low = parts(x)
    rest = (x - high.astype(F32) - low.astype(F32)).astype(BF16)
    count = x.shape[1] // BLOCK
    blocks = [slice(i * BLOCK, (i + 1) * BLOCK) for i in range(count)]
    sums = [dot(high[:, at], ones, 1, 0) + (dot(low[:, at], ones, 1, 0) + dot(rest[:, at], ones, 1, 0)) for at in blocks]
    carry = None
    for i in reversed(range(count)) if reverse else range(count):
        if carry is not None:
            sums[i] = sums[i] + carry
        carry = sums[i][:, :1] if reverse else sums[i][:, BLOCK - 1 :]
    return jnp.concatenate(sums, axis=1)


def head_rows(heads, channels):
    row = lax.broadcasted_iota(jnp.int32, (8, channels), 0)
    lane = lax.broadcasted_iota(jnp.int32, (8, channels), 1)
    return jnp.where(row // (8 // heads) == lane // (channels // heads), 1.0, 0.0).astype(BF16)


def store_rows(ref, value):
    size, width = value.shape
    count = width // BLOCK
    for j in range(count):
        ref[pl.ds(j, size, stride=count), :] = value[:, j * BLOCK : (j + 1) * BLOCK]


def spread_rows(x, heads, rows):
    return jnp.concatenate(
        [jnp.broadcast_to(x[k : k + 1], (rows // heads, x.shape[1])) for k in range(heads)], axis=0
    )


def first_kernel(heads, *refs):
    decay_hbm, b_hbm, c_hbm, g_hbm, w_hbm = refs[:5]
    pay_ref, run_ref, row_ref, eg_ref, b_ref, c_ref, g_ref, w_ref = refs[5:13]
    decay_ref, sems = refs[13:]
    half = w_ref.shape[0]
    side = lax.axis_index("groups") if half < w_hbm.shape[0] else 0
    pairs = (
        (decay_hbm, decay_ref),
        (g_hbm, g_ref),
        (c_hbm, c_ref),
        (w_hbm.at[pl.ds(pl.multiple_of(side * half, half), half), :], w_ref),
        (b_hbm, b_ref),
    )
    copies = [pltpu.make_async_copy(source, target, sems.at[i]) for i, (source, target) in enumerate(pairs)]
    for copy in copies:
        copy.start()
    copies[0].wait()
    channels = g_ref.shape[1]
    rows = scan_lanes(spread_rows(decay_ref[...], heads, 8), False)
    row_ref[...] = rows
    wide = jnp.concatenate(
        [jnp.broadcast_to(rows[k * 8 // heads : k * 8 // heads + 1], (channels // heads, rows.shape[1])) for k in range(heads)],
        axis=0,
    )
    run = wide.T
    run_ref[...] = run
    grow = jnp.exp(run)
    copies[1].wait()
    carried = grow * g_ref[...].astype(F32)
    eg_ref[...] = carried
    copies[2].wait()
    start = dot_right(c_ref[...], carried, 0, 0)
    state, tail = payload(start, jnp.exp(run[-1:, :]))
    n = state.shape[0]
    pay_ref[0:n, :] = state
    pay_ref[n : n + EXTRA, :] = tail
    for copy in copies[3:]:
        copy.wait()


def weights(run, rows, k, heads, width, lo, hi, size):
    column = run[lo:hi, k * width : k * width + 1]
    line = rows[k * 8 // heads : k * 8 // heads + 1, lo:size]
    spread = line - column
    s = lax.broadcasted_iota(jnp.int32, spread.shape, 0)
    t = lax.broadcasted_iota(jnp.int32, spread.shape, 1)
    return jnp.exp(jnp.where(t >= s, spread, -jnp.inf))


def local_kernel(heads, b_ref, c_ref, g_ref, run_ref, row_ref, q_ref, *near):
    for ref, source in zip(near, (b_ref, c_ref, g_ref, run_ref, row_ref)):
        ref[...] = source[...]
    size, channels = g_ref.shape
    width = channels // heads
    run, rows = run_ref[...], row_ref[...]
    for lo in range(0, size, BLOCK):
        hi = lo + BLOCK
        scores = dot(b_ref[lo:hi, :], c_ref[lo:size, :], 1, 1)
        out = []
        for k in range(heads):
            mixing = (scores * weights(run, rows, k, heads, width, lo, hi, size)).astype(BF16)
            out.append(dot(mixing, g_ref[lo:size, k * width : (k + 1) * width], 1, 0))
        q_ref[lo:hi, :] = jnp.concatenate(out, axis=1).astype(BF16)


def product(hid_ref, gx, index, rows):
    block = hid_ref[:, pl.ds(pl.multiple_of(index * rows, rows), rows)]
    return dot(gx, block, 0, 0).T


def grad_x_kernel(count, flip, hid_ref, *refs):
    pays, (b_ref, run_ref, q_ref), (ge_ref, bg_ref, gx_ref, out_ref) = (
        refs[:count],
        refs[count : count + 3],
        refs[count + 3 :],
    )
    ge = combine(pays, ge_ref.shape[0])
    ge_ref[...] = ge
    bg = dot_right(b_ref[...], ge, 1, 0)
    bg_ref[...] = bg
    run = run_ref[...]
    tail = jnp.exp(run[-1:, :] - run)
    gx = (q_ref[...].astype(F32) + tail * bg).astype(BF16)
    gx_ref[...] = gx
    out_ref[...] = product(hid_ref, gx, lax.axis_index("seq") ^ flip, out_ref.shape[0]).astype(out_ref.dtype)


def chunk_kernel(adds, flip, hid_ref, gx_ref, *refs):
    total = product(hid_ref, gx_ref[...], lax.axis_index("seq") ^ flip, refs[adds].shape[0])
    for ref in refs[:adds]:
        total = total + ref[...].astype(F32)
    refs[adds][...] = total.astype(refs[adds].dtype)


def fresh_payload(x, b, run, pay_ref):
    tail = jnp.exp(run[-1:, :] - run)
    fresh = dot_right(b, tail * x.astype(F32), 0, 0)
    state, extra = payload(fresh, jnp.exp(run[-1:, :]))
    n = state.shape[0]
    pay_ref[0:n, :] = state
    pay_ref[n : n + EXTRA, :] = extra


def proj_kernel(hops, swapped, last, hid_ref, *refs):
    count = len(hops)
    place, side, sections = lax.axis_index("seq"), lax.axis_index("groups"), lax.axis_size("seq")
    w_refs, rest = refs[:count], refs[count:]
    total = None if not last else rest[0][...]
    for ref, hop in zip(w_refs, hops):
        width = ref.shape[0]
        if hop == 0:
            at = place
        else:
            at = 2 * lax.rem(place - hop + sections, sections) + (1 - side if swapped else side)
        block = hid_ref[:, pl.ds(pl.multiple_of(at * width, width), width)]
        term = dot(block, ref[...], 1, 0)
        total = term if total is None else total + term
    if not last:
        rest[0][...] = total
    else:
        b_ref, run_ref, x_ref, pay_ref = rest[1:]
        x = total.astype(BF16)
        x_ref[...] = x
        fresh_payload(x, b_ref[...], run_ref[...], pay_ref)


def fresh_kernel(x_ref, b_ref, run_ref, pay_ref):
    fresh_payload(x_ref[...], b_ref[...], run_ref[...], pay_ref)


def section_kernel(heads, b_ref, c_ref, g_ref, x_ref, run_ref, row_ref, ge_ref, bg_ref, out_ref, gc_ref, gr_ref, gb_ref):
    size, channels = g_ref.shape
    width = channels // heads
    run, rows = run_ref[...], row_ref[...]
    x = x_ref[...].astype(F32)
    tail = jnp.exp(run[-1:, :] - run)
    moved = tail * x
    inner = moved * bg_ref[...]
    col = [[] for _ in range(heads)]
    line = [jnp.zeros((1, size), F32) for _ in range(heads)]
    gc_ref[...] = jnp.zeros_like(gc_ref)
    for lo in range(0, size, BLOCK):
        hi = lo + BLOCK
        scores = dot(b_ref[lo:hi, :], c_ref[lo:size, :], 1, 1)
        total = None
        for k in range(heads):
            ch = slice(k * width, (k + 1) * width)
            d_mix = dot(x_ref[lo:hi, ch], g_ref[lo:size, ch], 1, 1).astype(BF16).astype(F32)
            d_score = d_mix * weights(run, rows, k, heads, width, lo, hi, size)
            total = d_score if total is None else total + d_score
            z = d_score * scores
            col[k].append(jnp.sum(z, axis=1, keepdims=True))
            above = jnp.sum(z, axis=0, keepdims=True)
            if lo:
                above = jnp.concatenate([jnp.zeros((1, lo), F32), above], axis=1)
            line[k] = line[k] + above
        high, low = parts(total)
        gb_ref[lo:hi, :] = dot(high, c_ref[lo:size, :], 1, 0) + dot(low, c_ref[lo:size, :], 1, 0)
        gc_ref[lo:size, :] += dot(high, b_ref[lo:hi, :], 0, 0) + dot(low, b_ref[lo:hi, :], 0, 0)
    store_rows(out_ref, gb_ref[...] + dot_full(moved, ge_ref[...], 1, 1))
    picks = head_rows(heads, channels)
    fade = dot_right(picks, inner, 1, 1)
    lane = lax.broadcasted_iota(jnp.int32, (8, size), 1)
    taken = fade + jnp.concatenate(
        [jnp.broadcast_to(jnp.concatenate(part, axis=0), (size, 8 // heads)) for part in col], axis=1
    ).T
    given = jnp.concatenate([jnp.broadcast_to(part, (8 // heads, size)) for part in line], axis=0)
    gr_ref[...] = given - taken + jnp.where(lane == size - 1, jnp.sum(fade, axis=1, keepdims=True), 0.0)


def last_kernel(heads, count, *refs):
    pays = refs[:count]
    c_ref, eg_ref, run_ref, ge_ref, gc_ref, gr_ref, out_ref, gd_ref = refs[count:]
    size, channels = eg_ref.shape
    state = combine(pays, ge_ref.shape[0])
    carried = eg_ref[...]
    picks = head_rows(heads, channels)
    inner = carried * dot_right(c_ref[...], state, 1, 0)
    ends = jnp.exp(run_ref[size - 1 : size, :]) * jnp.sum(ge_ref[...] * state, axis=0, keepdims=True)
    last = jnp.sum(ends * picks.astype(F32), axis=1, keepdims=True)
    lane = lax.broadcasted_iota(jnp.int32, (8, size), 1)
    lines = dot_right(picks, inner, 1, 1) + gr_ref[...] + jnp.where(lane == size - 1, last, 0.0)
    total = scan_lanes(lines, True)
    for k in range(heads):
        gd_ref[k : k + 1, :] = total[k * 8 // heads : k * 8 // heads + 1, :]
    store_rows(out_ref, gc_ref[...] + dot_full(carried, state, 1, 1))


def shift(x, count, k):
    return lax.ppermute(x, "seq", [(i, i + k) for i in range(count) if 0 <= i + k < count])


def on_chip(kernel, shapes, flops, *args, far=(), scratch=(), limit=12):
    spaces = [pltpu.HBM if i in far else pltpu.VMEM for i in range(len(args))]
    many = isinstance(shapes, (list, tuple))
    vmem = pl.BlockSpec(memory_space=pltpu.VMEM)
    return pl.pallas_call(
        kernel,
        in_specs=[pl.BlockSpec(memory_space=m) for m in spaces],
        out_specs=[vmem] * len(shapes) if many else vmem,
        out_shape=list(shapes) if many else shapes,
        scratch_shapes=list(scratch),
        compiler_params=params(limit),
        cost_estimate=cost(int(flops * 1.1e9), 1 << 10),
    )(*args)


def body(hidden, w_in, decay_log, b_proj, c_proj, grad_out):
    count = lax.axis_size("seq")
    size, heads = decay_log.shape
    channels = w_in.shape[1]
    states = b_proj.shape[2]
    share = w_in.shape[0]
    b = b_proj.reshape(size, states)
    c = c_proj.reshape(size, states)
    f32 = lambda *s: jax.ShapeDtypeStruct(s, F32)
    b16 = lambda *s: jax.ShapeDtypeStruct(s, BF16)

    direct = count == 4 and lax.axis_size("groups") == 2
    half = share // 2 if direct else share
    pay, run, rows, eg, b, c, g, mine = on_chip(
        functools.partial(first_kernel, heads),
        (
            b16(states + EXTRA, channels),
            f32(size, channels),
            f32(8, size),
            f32(size, channels),
            b16(size, states),
            b16(size, states),
            b16(size, channels),
            b16(half, channels),
        ),
        1.2, decay_log.T, b, c, grad_out, w_in,
        far=range(5), limit=54, scratch=[pltpu.VMEM((heads, size), F32), pltpu.SemaphoreType.DMA((5,))],
    )
    later = [shift(pay, count, -k) for k in range(1, count)]

    if direct:
        hops = (2, 1, 3)
        moved = [lax.ppermute(mine, "seq", [(i, (i + k) % count) for i in range(count)]) for k in hops]
        other = [lax.ppermute(m, "groups", [(0, 1), (1, 0)]) for m in moved]

    q, b, c, g, run, rows = on_chip(
        functools.partial(local_kernel, heads),
        (b16(size, channels), b16(size, states), b16(size, states), b16(size, channels), f32(size, channels), f32(8, size)),
        1.1, b, c, g, run, rows,
    )
    ge, bg, gx, send_a = on_chip(
        functools.partial(grad_x_kernel, count - 1, 3 if direct else 0),
        (f32(states, channels), f32(size, channels), b16(size, channels), b16(share, channels)),
        8.0, hidden, *later, b, run, q,
    )

    if direct:
        near = [(i, i ^ 1) for i in range(count)]
        far = [(i, i ^ 2) for i in range(count)]
        chunk = lambda flip, dtype, price, *adds: on_chip(
            functools.partial(chunk_kernel, len(adds), flip),
            jax.ShapeDtypeStruct((share, channels), dtype),
            price, hidden, gx, *adds,
        )
        got_a = lax.ppermute(send_a, "seq", near)
        send_b = chunk(1, BF16, 6.0)
        got_b = lax.ppermute(send_b, "seq", near)
        send_c = chunk(2, BF16, 6.0, got_a)
        got_c = lax.ppermute(send_c, "seq", far)
        own = chunk(0, F32, 0.55, got_b)

        acc = on_chip(
            functools.partial(proj_kernel, (0,) + hops, False, False),
            f32(size, channels),
            1.5, hidden, w_in, *moved,
        )
        x, pay_x = on_chip(
            functools.partial(proj_kernel, hops, True, True),
            (b16(size, channels), b16(states + EXTRA, channels)),
            1.5, hidden, *other, acc, b, run,
        )
    else:
        grad_w = lax.psum_scatter(
            lax.dot_general(hidden, gx, (((0,), (0,)), ((), ())), preferred_element_type=F32),
            "seq",
            scatter_dimension=0,
            tiled=True,
        )
        w_all = lax.all_gather(w_in, "seq", axis=0, tiled=True)
        x = jnp.dot(hidden, w_all, preferred_element_type=F32).astype(BF16)
        pay_x = on_chip(fresh_kernel, b16(states + EXTRA, channels), 1.0, x, b, run)

    earlier = [shift(pay_x, count, k) for k in range(1, count)]
    flat = size * states // BLOCK
    grad_b, gc_part, gr_part = on_chip(
        functools.partial(section_kernel, heads),
        (f32(flat, BLOCK), f32(size, states), f32(8, size)),
        1.8, b, c, g, x, run, rows, ge, bg, scratch=[pltpu.VMEM((size, states), F32)],
    )
    if direct:
        gc_part, own = lax.optimization_barrier((gc_part, own))
    grad_c, grad_decay = on_chip(
        functools.partial(last_kernel, heads, count - 1),
        (f32(flat, BLOCK), f32(heads, size)),
        2.6, *earlier, c, eg, run, ge, gc_part, gr_part,
    )
    if direct:
        grad_w = own + got_c.astype(F32)
    return (
        grad_w,
        grad_decay.T,
        grad_b.reshape(size, 1, states),
        grad_c.reshape(size, 1, states),
    )


def solution(mesh):
    return jax.shard_map(
        body,
        mesh=mesh,
        in_specs=(
            P(("groups", "seq"), None),
            P("seq", "head"),
            P(("groups", "seq"), "head"),
            P(("groups", "seq"), "head", None),
            P(("groups", "seq"), "head", None),
            P(("groups", "seq"), "head"),
        ),
        out_specs=(
            P(("groups", "seq"), "head"),
            P(("groups", "seq"), "head"),
            P(("groups", "seq"), "head", None),
            P(("groups", "seq"), "head", None),
        ),
        check_vma=False,
    )
```

```python
import functools
import jax
import jax.numpy as jnp
from jax import lax
from jax.experimental import pallas as pl
from jax.experimental.pallas import tpu as pltpu
from jax.sharding import PartitionSpec as P

F32 = jnp.float32
BF16 = jnp.bfloat16
EXTRA = 16
BLOCK = 128


def params(limit=12):
    return pltpu.CompilerParams(vmem_limit_bytes=limit << 20)


def cost(flops, moved, exps=0):
    return pl.CostEstimate(flops=flops, bytes_accessed=moved, transcendentals=exps)


def dot(a, b, ca, cb):
    return lax.dot_general(a, b, (((ca,), (cb,)), ((), ())), preferred_element_type=F32)


def parts(x):
    high = x.astype(BF16)
    return high, (x - high.astype(F32)).astype(BF16)


def dot_left(x, b, ca, cb):
    high, low = parts(x)
    return dot(high, b, ca, cb) + dot(low, b, ca, cb)


def dot_right(a, x, ca, cb):
    high, low = parts(x)
    return dot(a, high, ca, cb) + dot(a, low, ca, cb)


def dot_full(x, y, ca, cb):
    xh, xl = parts(x)
    yh, yl = parts(y)
    return dot(xh, yh, ca, cb) + (dot(xh, yl, ca, cb) + dot(xl, yh, ca, cb))


def payload(state, last):
    high = last.astype(BF16).astype(F32)
    mid = (last - high).astype(BF16).astype(F32)
    low = last - high - mid
    row = lax.broadcasted_iota(jnp.int32, (EXTRA, last.shape[1]), 0)
    tail = jnp.where(row == 0, high, jnp.where(row == 1, mid, jnp.where(row == 2, low, 0.0)))
    return state.astype(BF16), tail.astype(BF16)


def combine(refs, rows):
    total = None
    for ref in reversed(refs):
        state = ref[0:rows, :].astype(F32)
        if total is not None:
            deep = ref[rows : rows + EXTRA, :].astype(F32)
            state = state + (deep[0:1] + deep[1:2] + deep[2:3]) * total
        total = state
    return total


def scan_lanes(x, reverse):
    row = lax.broadcasted_iota(jnp.int32, (BLOCK, BLOCK), 0)
    lane = lax.broadcasted_iota(jnp.int32, (BLOCK, BLOCK), 1)
    ones = jnp.where(row >= lane if reverse else row <= lane, 1.0, 0.0).astype(BF16)
    high, low = parts(x)
    rest = (x - high.astype(F32) - low.astype(F32)).astype(BF16)
    count = x.shape[1] // BLOCK
    blocks = [slice(i * BLOCK, (i + 1) * BLOCK) for i in range(count)]
    sums = [dot(high[:, at], ones, 1, 0) + (dot(low[:, at], ones, 1, 0) + dot(rest[:, at], ones, 1, 0)) for at in blocks]
    carry = None
    for i in reversed(range(count)) if reverse else range(count):
        if carry is not None:
            sums[i] = sums[i] + carry
        carry = sums[i][:, :1] if reverse else sums[i][:, BLOCK - 1 :]
    return jnp.concatenate(sums, axis=1)


def head_rows(heads, channels):
    row = lax.broadcasted_iota(jnp.int32, (8, channels), 0)
    lane = lax.broadcasted_iota(jnp.int32, (8, channels), 1)
    return jnp.where(row // (8 // heads) == lane // (channels // heads), 1.0, 0.0).astype(BF16)


def store_rows(ref, value):
    size, width = value.shape
    count = width // BLOCK
    for j in range(count):
        ref[pl.ds(j, size, stride=count), :] = value[:, j * BLOCK : (j + 1) * BLOCK]


def spread_rows(x, heads, rows):
    return jnp.concatenate(
        [jnp.broadcast_to(x[k : k + 1], (rows // heads, x.shape[1])) for k in range(heads)], axis=0
    )


def first_kernel(heads, *refs):
    decay_hbm, b_hbm, c_hbm, g_hbm, w_hbm = refs[:5]
    pay_ref, run_ref, row_ref, eg_ref, b_ref, c_ref, g_ref, w_ref = refs[5:13]
    decay_ref, sems = refs[13:]
    half = w_ref.shape[0]
    side = lax.axis_index("groups") if half < w_hbm.shape[0] else 0
    pairs = (
        (decay_hbm, decay_ref),
        (g_hbm, g_ref),
        (c_hbm, c_ref),
        (w_hbm.at[pl.ds(pl.multiple_of(side * half, half), half), :], w_ref),
        (b_hbm, b_ref),
    )
    copies = [pltpu.make_async_copy(source, target, sems.at[i]) for i, (source, target) in enumerate(pairs)]
    for copy in copies:
        copy.start()
    copies[0].wait()
    channels = g_ref.shape[1]
    rows = scan_lanes(spread_rows(decay_ref[...], heads, 8), False)
    row_ref[...] = rows
    wide = jnp.concatenate(
        [jnp.broadcast_to(rows[k * 8 // heads : k * 8 // heads + 1], (channels // heads, rows.shape[1])) for k in range(heads)],
        axis=0,
    )
    run = wide.T
    run_ref[...] = run
    grow = jnp.exp(run)
    copies[1].wait()
    carried = grow * g_ref[...].astype(F32)
    eg_ref[...] = carried
    copies[2].wait()
    start = dot_right(c_ref[...], carried, 0, 0)
    state, tail = payload(start, jnp.exp(run[-1:, :]))
    n = state.shape[0]
    pay_ref[0:n, :] = state
    pay_ref[n : n + EXTRA, :] = tail
    for copy in copies[3:]:
        copy.wait()


def weights(run, rows, k, heads, width, lo, hi, size):
    column = run[lo:hi, k * width : k * width + 1]
    line = rows[k * 8 // heads : k * 8 // heads + 1, lo:size]
    spread = line - column
    s = lax.broadcasted_iota(jnp.int32, spread.shape, 0)
    t = lax.broadcasted_iota(jnp.int32, spread.shape, 1)
    return jnp.exp(jnp.where(t >= s, spread, -jnp.inf))


def local_kernel(heads, b_ref, c_ref, g_ref, run_ref, row_ref, q_ref, *near):
    for ref, source in zip(near, (b_ref, c_ref, g_ref, run_ref, row_ref)):
        ref[...] = source[...]
    size, channels = g_ref.shape
    width = channels // heads
    run, rows = run_ref[...], row_ref[...]
    for lo in range(0, size, BLOCK):
        hi = lo + BLOCK
        scores = dot(b_ref[lo:hi, :], c_ref[lo:size, :], 1, 1)
        out = []
        for k in range(heads):
            mixing = (scores * weights(run, rows, k, heads, width, lo, hi, size)).astype(BF16)
            out.append(dot(mixing, g_ref[lo:size, k * width : (k + 1) * width], 1, 0))
        q_ref[lo:hi, :] = jnp.concatenate(out, axis=1).astype(BF16)


def product(hid_ref, gx, index, rows):
    block = hid_ref[:, pl.ds(pl.multiple_of(index * rows, rows), rows)]
    return dot(gx, block, 0, 0).T


def grad_x_kernel(count, flip, hid_ref, *refs):
    pays, (b_ref, run_ref, q_ref), (ge_ref, bg_ref, gx_ref, *outs) = (
        refs[:count],
        refs[count : count + 3],
        refs[count + 3 :],
    )
    ge = combine(pays, ge_ref.shape[0])
    ge_ref[...] = ge
    bg = dot_right(b_ref[...], ge, 1, 0)
    bg_ref[...] = bg
    run = run_ref[...]
    tail = jnp.exp(run[-1:, :] - run)
    gx = (q_ref[...].astype(F32) + tail * bg).astype(BF16)
    gx_ref[...] = gx
    for piece, ref in enumerate(outs):
        index = (lax.axis_index("seq") ^ flip) * len(outs) + piece
        ref[...] = product(hid_ref, gx, index, ref.shape[0]).astype(ref.dtype)


def chunk_kernel(adds, flip, pieces, piece, hid_ref, gx_ref, *refs):
    total = product(hid_ref, gx_ref[...], (lax.axis_index("seq") ^ flip) * pieces + piece, refs[adds].shape[0])
    for ref in refs[:adds]:
        total = total + ref[...].astype(F32)
    refs[adds][...] = total.astype(refs[adds].dtype)


def fresh_payload(x, b, run, pay_ref):
    tail = jnp.exp(run[-1:, :] - run)
    fresh = dot_right(b, tail * x.astype(F32), 0, 0)
    state, extra = payload(fresh, jnp.exp(run[-1:, :]))
    n = state.shape[0]
    pay_ref[0:n, :] = state
    pay_ref[n : n + EXTRA, :] = extra


def proj_kernel(hops, swapped, last, hid_ref, *refs):
    count = len(hops)
    place, side, sections = lax.axis_index("seq"), lax.axis_index("groups"), lax.axis_size("seq")
    w_refs, rest = refs[:count], refs[count:]
    total = None if not last else rest[0][...]
    for ref, hop in zip(w_refs, hops):
        width = ref.shape[0]
        if hop == 0:
            at = place
        else:
            at = 2 * lax.rem(place - hop + sections, sections) + (1 - side if swapped else side)
        block = hid_ref[:, pl.ds(pl.multiple_of(at * width, width), width)]
        term = dot(block, ref[...], 1, 0)
        total = term if total is None else total + term
    if not last:
        rest[0][...] = total
    else:
        b_ref, run_ref, x_ref, pay_ref = rest[1:]
        x = total.astype(BF16)
        x_ref[...] = x
        fresh_payload(x, b_ref[...], run_ref[...], pay_ref)


def fresh_kernel(x_ref, b_ref, run_ref, pay_ref):
    fresh_payload(x_ref[...], b_ref[...], run_ref[...], pay_ref)


def section_kernel(heads, b_ref, c_ref, g_ref, x_ref, run_ref, row_ref, ge_ref, bg_ref, out_ref, gc_ref, gr_ref, gb_ref):
    size, channels = g_ref.shape
    width = channels // heads
    run, rows = run_ref[...], row_ref[...]
    x = x_ref[...].astype(F32)
    tail = jnp.exp(run[-1:, :] - run)
    moved = tail * x
    inner = moved * bg_ref[...]
    col = [[] for _ in range(heads)]
    line = [jnp.zeros((1, size), F32) for _ in range(heads)]
    gc_ref[...] = jnp.zeros_like(gc_ref)
    for lo in range(0, size, BLOCK):
        hi = lo + BLOCK
        scores = dot(b_ref[lo:hi, :], c_ref[lo:size, :], 1, 1)
        total = None
        for k in range(heads):
            ch = slice(k * width, (k + 1) * width)
            d_mix = dot(x_ref[lo:hi, ch], g_ref[lo:size, ch], 1, 1).astype(BF16).astype(F32)
            d_score = d_mix * weights(run, rows, k, heads, width, lo, hi, size)
            total = d_score if total is None else total + d_score
            z = d_score * scores
            col[k].append(jnp.sum(z, axis=1, keepdims=True))
            above = jnp.sum(z, axis=0, keepdims=True)
            if lo:
                above = jnp.concatenate([jnp.zeros((1, lo), F32), above], axis=1)
            line[k] = line[k] + above
        high, low = parts(total)
        gb_ref[lo:hi, :] = dot(high, c_ref[lo:size, :], 1, 0) + dot(low, c_ref[lo:size, :], 1, 0)
        gc_ref[lo:size, :] += dot(high, b_ref[lo:hi, :], 0, 0) + dot(low, b_ref[lo:hi, :], 0, 0)
    store_rows(out_ref, gb_ref[...] + dot_full(moved, ge_ref[...], 1, 1))
    picks = head_rows(heads, channels)
    fade = dot_right(picks, inner, 1, 1)
    lane = lax.broadcasted_iota(jnp.int32, (8, size), 1)
    taken = fade + jnp.concatenate(
        [jnp.broadcast_to(jnp.concatenate(part, axis=0), (size, 8 // heads)) for part in col], axis=1
    ).T
    given = jnp.concatenate([jnp.broadcast_to(part, (8 // heads, size)) for part in line], axis=0)
    gr_ref[...] = given - taken + jnp.where(lane == size - 1, jnp.sum(fade, axis=1, keepdims=True), 0.0)


def last_kernel(heads, count, *refs):
    pays = refs[:count]
    c_ref, eg_ref, run_ref, ge_ref, gc_ref, gr_ref, out_ref, gd_ref = refs[count:]
    size, channels = eg_ref.shape
    state = combine(pays, ge_ref.shape[0])
    carried = eg_ref[...]
    picks = head_rows(heads, channels)
    inner = carried * dot_right(c_ref[...], state, 1, 0)
    ends = jnp.exp(run_ref[size - 1 : size, :]) * jnp.sum(ge_ref[...] * state, axis=0, keepdims=True)
    last = jnp.sum(ends * picks.astype(F32), axis=1, keepdims=True)
    lane = lax.broadcasted_iota(jnp.int32, (8, size), 1)
    lines = dot_right(picks, inner, 1, 1) + gr_ref[...] + jnp.where(lane == size - 1, last, 0.0)
    total = scan_lanes(lines, True)
    for k in range(heads):
        gd_ref[k : k + 1, :] = total[k * 8 // heads : k * 8 // heads + 1, :]
    store_rows(out_ref, gc_ref[...] + dot_full(carried, state, 1, 1))


def shift(x, count, k):
    return lax.ppermute(x, "seq", [(i, i + k) for i in range(count) if 0 <= i + k < count])


def on_chip(kernel, shapes, flops, *args, far=(), scratch=(), limit=12):
    spaces = [pltpu.HBM if i in far else pltpu.VMEM for i in range(len(args))]
    many = isinstance(shapes, (list, tuple))
    vmem = pl.BlockSpec(memory_space=pltpu.VMEM)
    return pl.pallas_call(
        kernel,
        in_specs=[pl.BlockSpec(memory_space=m) for m in spaces],
        out_specs=[vmem] * len(shapes) if many else vmem,
        out_shape=list(shapes) if many else shapes,
        scratch_shapes=list(scratch),
        compiler_params=params(limit),
        cost_estimate=cost(int(flops * 1.1e9), 1 << 10),
    )(*args)


def body(hidden, w_in, decay_log, b_proj, c_proj, grad_out):
    count = lax.axis_size("seq")
    size, heads = decay_log.shape
    channels = w_in.shape[1]
    states = b_proj.shape[2]
    share = w_in.shape[0]
    b = b_proj.reshape(size, states)
    c = c_proj.reshape(size, states)
    f32 = lambda *s: jax.ShapeDtypeStruct(s, F32)
    b16 = lambda *s: jax.ShapeDtypeStruct(s, BF16)

    direct = count == 4 and lax.axis_size("groups") == 2
    half = share // 2 if direct else share
    pay, run, rows, eg, b, c, g, mine = on_chip(
        functools.partial(first_kernel, heads),
        (
            b16(states + EXTRA, channels),
            f32(size, channels),
            f32(8, size),
            f32(size, channels),
            b16(size, states),
            b16(size, states),
            b16(size, channels),
            b16(half, channels),
        ),
        1.2, decay_log.T, b, c, grad_out, w_in,
        far=range(5), limit=54, scratch=[pltpu.VMEM((heads, size), F32), pltpu.SemaphoreType.DMA((5,))],
    )
    later = [shift(pay, count, -k) for k in range(1, count)]

    if direct:
        hops = (2, 1, 3)
        moved = [lax.ppermute(mine, "seq", [(i, (i + k) % count) for i in range(count)]) for k in hops]
        other = [lax.ppermute(m, "groups", [(0, 1), (1, 0)]) for m in moved]

    q, b, c, g, run, rows = on_chip(
        functools.partial(local_kernel, heads),
        (b16(size, channels), b16(size, states), b16(size, states), b16(size, channels), f32(size, channels), f32(8, size)),
        1.1, b, c, g, run, rows,
    )
    cut = 2 if direct else 1
    ge, bg, gx, *send_a = on_chip(
        functools.partial(grad_x_kernel, count - 1, 3 if direct else 0),
        (f32(states, channels), f32(size, channels), b16(size, channels)) + (b16(share // cut, channels),) * cut,
        8, hidden, *later, b, run, q,
    )

    if direct:
        near = [(i, i ^ 1) for i in range(count)]
        far = [(i, i ^ 2) for i in range(count)]
        chunk = lambda flip, dtype, price, gx, *adds, pieces=1, piece=0: on_chip(
            functools.partial(chunk_kernel, len(adds), flip, pieces, piece),
            jax.ShapeDtypeStruct((share // pieces, channels), dtype),
            price, hidden, gx, *adds,
        )
        got_a = [lax.ppermute(part, "seq", near) for part in send_a]
        send_c = [chunk(2, BF16, 6, gx, part, pieces=cut, piece=i) for i, part in enumerate(got_a)]
        got_c = [lax.ppermute(part, "seq", far) for part in send_c]
        send_b = chunk(1, BF16, 6, gx)
        got_b = lax.ppermute(send_b, "seq", near)
        own = chunk(0, F32, 2, gx, got_b)

        acc = on_chip(
            functools.partial(proj_kernel, (0,) + hops, False, False),
            f32(size, channels),
            12, hidden, w_in, *moved,
        )
        x, pay_x = on_chip(
            functools.partial(proj_kernel, hops, True, True),
            (b16(size, channels), b16(states + EXTRA, channels)),
            1, hidden, *other, acc, b, run,
        )
    else:
        grad_w = lax.psum_scatter(
            lax.dot_general(hidden, gx, (((0,), (0,)), ((), ())), preferred_element_type=F32),
            "seq",
            scatter_dimension=0,
            tiled=True,
        )
        w_all = lax.all_gather(w_in, "seq", axis=0, tiled=True)
        x = jnp.dot(hidden, w_all, preferred_element_type=F32).astype(BF16)
        pay_x = on_chip(fresh_kernel, b16(states + EXTRA, channels), 1.0, x, b, run)

    earlier = [shift(pay_x, count, k) for k in range(1, count)]
    flat = size * states // BLOCK
    grad_b, gc_part, gr_part = on_chip(
        functools.partial(section_kernel, heads),
        (f32(flat, BLOCK), f32(size, states), f32(8, size)),
        3, b, c, g, x, run, rows, ge, bg, scratch=[pltpu.VMEM((size, states), F32)],
    )
    if direct:
        gc_part, own = lax.optimization_barrier((gc_part, own))
    grad_c, grad_decay = on_chip(
        functools.partial(last_kernel, heads, count - 1),
        (f32(flat, BLOCK), f32(heads, size)),
        12, *earlier, c, eg, run, ge, gc_part, gr_part,
    )
    if direct:
        grad_w = own + jnp.concatenate(got_c, axis=0).astype(F32)
    return (
        grad_w,
        grad_decay.T,
        grad_b.reshape(size, 1, states),
        grad_c.reshape(size, 1, states),
    )


def solution(mesh):
    return jax.shard_map(
        body,
        mesh=mesh,
        in_specs=(
            P(("groups", "seq"), None),
            P("seq", "head"),
            P(("groups", "seq"), "head"),
            P(("groups", "seq"), "head", None),
            P(("groups", "seq"), "head", None),
            P(("groups", "seq"), "head"),
        ),
        out_specs=(
            P(("groups", "seq"), "head"),
            P(("groups", "seq"), "head"),
            P(("groups", "seq"), "head", None),
            P(("groups", "seq"), "head", None),
        ),
        check_vma=False,
    )
```
